32 devices in a mesh: seq: 8 (over z, y), tp: 4 (over x, core).
Axes of the slice: x: 2, y: 2, z: 4, core: 2. Of those that a mesh axis runs over, the one named last changes fastest.
Arguments:
- x_in: float32 [2, 1024, 1024], P(None, 'seq'), may hold values from -6 to 6
- cotangent: float32 [2, 1024, 1024], P(None, 'seq'), may hold values from -6 to 6
- conv_gain: float32 [1024], replicated, may hold values from 0.5 to 1.5
- conv_input: bfloat16 [1024, 3, 1024], P(None, None, 'tp'), may hold values from -0.1875 to 0.1875
- conv_kernel: float32 [3, 1024], P(None, 'tp'), may hold values from -3 to 3
- conv_output: bfloat16 [1024, 1024], P('tp'), may hold values from -0.1875 to 0.1875
- feed_gain_a: float32 [1024], replicated, may hold values from 0.5 to 1.5
- gate_first: bfloat16 [1024, 4608], P(None, 'tp'), may hold values from -0.1875 to 0.1875
- up_first: bfloat16 [1024, 4608], P(None, 'tp'), may hold values from -0.1875 to 0.1875
- down_first: bfloat16 [4608, 1024], P('tp'), may hold values from -0.09375 to 0.09375
- attend_gain: float32 [1024], replicated, may hold values from 0.5 to 1.5
- query_weight: bfloat16 [1024, 1024], P(None, 'tp'), may hold values from -0.1875 to 0.1875
- key_weight: bfloat16 [1024, 512], P(None, 'tp'), may hold values from -0.1875 to 0.1875
- value_weight: bfloat16 [1024, 512], P(None, 'tp'), may hold values from -0.1875 to 0.1875
- query_gain: float32 [64], replicated, may hold values from 0.5 to 1.5
- key_gain: float32 [64], replicated, may hold values from 0.5 to 1.5
- output_weight: bfloat16 [1024, 1024], P('tp'), may hold values from -1 to 1
- feed_gain_b: float32 [1024], replicated, may hold values from 0.5 to 1.5
- gate_second: bfloat16 [1024, 4608], P(None, 'tp'), may hold values from -0.1875 to 0.1875
- up_second: bfloat16 [1024, 4608], P(None, 'tp'), may hold values from -0.1875 to 0.1875
- down_second: bfloat16 [4608, 1024], P('tp'), may hold values from -0.09375 to 0.09375
Outputs:
- layer_out: float32 [2, 1024, 1024], P(None, 'seq')
- grad_input: float32 [2, 1024, 1024], P(None, 'seq')
- grad_conv_gain: float32 [1024], replicated
- grad_conv_input: float32 [1024, 3, 1024], P('seq', None, 'tp')
- grad_conv_kernel: float32 [3, 1024], replicated
- grad_conv_output: float32 [1024, 1024], P('tp', 'seq')
- grad_feed_gain_a: float32 [1024], replicated
- grad_gate_first: float32 [1024, 4608], P('seq', 'tp')
- grad_up_first: float32 [1024, 4608], P('seq', 'tp')
- grad_down_first: float32 [4608, 1024], P('tp', 'seq')
- grad_attend_gain: float32 [1024], replicated
- grad_query_weight: float32 [1024, 1024], P('seq', 'tp')
- grad_key_weight: float32 [1024, 512], P('seq', 'tp')
- grad_value_weight: float32 [1024, 512], P('seq', 'tp')
- grad_query_gain: float32 [64], replicated
- grad_key_gain: float32 [64], replicated
- grad_output_weight: float32 [1024, 1024], P('tp', 'seq')
- grad_feed_gain_b: float32 [1024], replicated
- grad_gate_second: float32 [1024, 4608], P('seq', 'tp')
- grad_up_second: float32 [1024, 4608], P('seq', 'tp')
- grad_down_second: float32 [4608, 1024], P('tp', 'seq')
The draws below stay inside these ranges and needn't reach their ends.
All inputs are finite; a program needn't handle non-finite values.
Results may differ from the reference program's by a relative error of at most 0.025.
Values may be sent and summed in bfloat16 or wider, within the bound.
No kernel may reach another device: no remote copies, remote signals or barrier semaphores. Data moves between devices by JAX's collectives and lax.ppermute only.
A program may use at most 192 MiB of HBM per device.

```python
import jax
import jax.numpy as jnp
from jax import lax

D = 1024
FF = 4608
H = 16
KVH = 8
HD = 64
SEQS = 2
LEN = 1024


def block_levels(own_key, shape, shards, least, largest):
    factor_of = 1.0
    for dim, blocks in shards:
        draws = jax.random.uniform(jax.random.fold_in(jax.random.fold_in(own_key, 6), dim), (blocks,), jnp.float32, least / len(shards), largest / len(shards))
        factor_of = factor_of * jnp.repeat(jnp.exp(draws), shape[dim] // blocks).reshape((-1,) + (1,) * (len(shape) - 1 - dim))
    return factor_of


def noise(rng, dims, scale, most, cuts=(), kind=jnp.bfloat16):
    values = scale * jax.random.normal(rng, dims, jnp.float32)
    if cuts:
        values = values * block_levels(rng, dims, cuts, -0.22, 0.18)
    return jnp.clip(values, -most, most).astype(kind)


def setup_inputs(seed: int = 0) -> dict:
    key_list = jax.random.split(jax.random.key(seed), 22)
    return {
        "x_in": noise(key_list[0], (SEQS, LEN, D), 1.0, 6.0, ((1, 8),), jnp.float32),
        "cotangent": noise(key_list[1], (SEQS, LEN, D), 1.0, 6.0, ((1, 8),), jnp.float32),
        "conv_gain": jnp.clip(1.0 + 0.1 * jax.random.normal(key_list[2], (D,), jnp.float32), 0.5, 1.5),
        "conv_input": noise(key_list[3], (D, 3, D), D ** -0.5, 0.1875, ((2, 4),)),
        "conv_kernel": noise(key_list[4], (3, D), 0.6, 3.0, ((1, 4),), jnp.float32),
        "conv_output": noise(key_list[5], (D, D), D ** -0.5, 0.1875, ((0, 4),)),
        "feed_gain_a": jnp.clip(1.0 + 0.1 * jax.random.normal(key_list[6], (D,), jnp.float32), 0.5, 1.5),
        "gate_first": noise(key_list[7], (D, FF), D ** -0.5, 0.1875, ((1, 4),)),
        "up_first": noise(key_list[8], (D, FF), D ** -0.5, 0.1875, ((1, 4),)),
        "down_first": noise(key_list[9], (FF, D), FF ** -0.5, 0.09375, ((0, 4),)),
        "attend_gain": jnp.clip(1.0 + 0.1 * jax.random.normal(key_list[10], (D,), jnp.float32), 0.5, 1.5),
        "query_weight": noise(key_list[11], (D, H * HD), D ** -0.5, 0.1875, ((1, 4),)),
        "key_weight": noise(key_list[12], (D, KVH * HD), D ** -0.5, 0.1875, ((1, 4),)),
        "value_weight": noise(key_list[13], (D, KVH * HD), D ** -0.5, 0.1875, ((1, 4),)),
        "query_gain": jnp.clip(1.0 + 0.1 * jax.random.normal(key_list[14], (HD,), jnp.float32), 0.5, 1.5),
        "key_gain": jnp.clip(1.0 + 0.1 * jax.random.normal(key_list[15], (HD,), jnp.float32), 0.5, 1.5),
        "output_weight": noise(key_list[16], (H * HD, D), 32 ** -0.5, 1.0, ((0, 4),)),
        "feed_gain_b": jnp.clip(1.0 + 0.1 * jax.random.normal(key_list[17], (D,), jnp.float32), 0.5, 1.5),
        "gate_second": noise(key_list[18], (D, FF), D ** -0.5, 0.1875, ((1, 4),)),
        "up_second": noise(key_list[19], (D, FF), D ** -0.5, 0.1875, ((1, 4),)),
        "down_second": noise(key_list[20], (FF, D), FF ** -0.5, 0.09375, ((0, 4),)),
    }


EPSILON = 1e-05
THETA = 1000000.0

def matmul(lhs_matrix, rhs_matrix):
    return jnp.dot(lhs_matrix, rhs_matrix, preferred_element_type=jnp.float32)

def left_product(lhs_matrix, rhs_matrix):
    return lax.dot_general(lhs_matrix, rhs_matrix, (((0,), (0,)), ((), ())), preferred_element_type=jnp.float32)

def right_product(lhs_matrix, rhs_matrix):
    return lax.dot_general(lhs_matrix, rhs_matrix, (((1,), (1,)), ((), ())), preferred_element_type=jnp.float32)

def norm_forward(stream, norm_gain):
    inv_rms = lax.rsqrt(lax.optimization_barrier(jnp.mean(stream * stream, axis=-1, keepdims=True)) + EPSILON)
    normed = stream * inv_rms
    return (normed, inv_rms, normed * norm_gain)

def norm_backward(grad_scaled, normed, inv_rms, norm_gain):
    grad_normed = grad_scaled * norm_gain
    grad_gain = lax.optimization_barrier(jnp.sum((grad_scaled * normed).reshape(-1, norm_gain.shape[0]), axis=0))
    grad_stream = inv_rms * (grad_normed - normed * lax.optimization_barrier(jnp.mean(grad_normed * normed, axis=-1, keepdims=True)))
    return (grad_stream, grad_gain)

def feed_forward(stream, norm_gain, gate_weight, up_weight, down_weight):
    normed, inv_rms, scaled = norm_forward(stream, norm_gain)
    scaled = scaled.astype(jnp.bfloat16)
    gate_pre = matmul(scaled, gate_weight)
    up_pre = matmul(scaled, up_weight)
    hidden = (gate_pre * jax.nn.sigmoid(gate_pre) * up_pre).astype(jnp.bfloat16)
    result = stream + matmul(hidden, down_weight)
    return (result, (normed, inv_rms, scaled, gate_pre, up_pre, hidden))

def feed_backward(grad_out, saved_state, norm_gain, gate_weight, up_weight, down_weight):
    normed, inv_rms, scaled, gate_pre, up_pre, hidden = saved_state
    grad_low = grad_out.astype(jnp.bfloat16)
    grad_down = left_product(hidden, grad_low)
    grad_hidden = right_product(grad_low, down_weight)
    sigmoid_gate = jax.nn.sigmoid(gate_pre)
    grad_gate = (grad_hidden * up_pre * sigmoid_gate * (1.0 + gate_pre * (1.0 - sigmoid_gate))).astype(jnp.bfloat16)
    grad_up = (grad_hidden * gate_pre * sigmoid_gate).astype(jnp.bfloat16)
    grad_scaled = right_product(grad_gate, gate_weight) + right_product(grad_up, up_weight)
    grad_stream, grad_gain = norm_backward(grad_scaled, normed, inv_rms, norm_gain)
    return (grad_out + grad_stream, grad_gain, (left_product(scaled, grad_gate), left_product(scaled, grad_up), grad_down))

def rope_tables(positions, head_dim):
    half_dim = head_dim // 2
    frequency = THETA ** (-(2.0 * jnp.arange(half_dim, dtype=jnp.float32)) / head_dim)
    angles = positions.astype(jnp.float32)[:, None] * frequency[None, :]
    cosine_table = jnp.concatenate([jnp.cos(angles), jnp.cos(angles)], axis=-1)
    sine_table = jnp.concatenate([jnp.sin(angles), jnp.sin(angles)], axis=-1)
    return (cosine_table, sine_table)

def rotate(field, cosine_table, sine_table):
    half_dim = field.shape[-1] // 2
    turned = jnp.concatenate([-field[..., half_dim:], field[..., :half_dim]], axis=-1)
    return field * cosine_table[:, None, :] + turned * sine_table[:, None, :]

def rotate_back(grad_field, cosine_table, sine_table):
    half_dim = grad_field.shape[-1] // 2
    moved = grad_field * sine_table[:, None, :]
    turned = jnp.concatenate([moved[..., half_dim:], -moved[..., :half_dim]], axis=-1)
    return grad_field * cosine_table[:, None, :] + turned

def attend_block(queries, key_rows, value_rows, first_pos, head_dim):
    row_count, head_count = (queries.shape[0], queries.shape[1])
    groups = key_rows.shape[1]
    grouped = queries.astype(jnp.float32).reshape(row_count, groups, head_count // groups, head_dim)
    scores = jnp.einsum('igkd,jgd->gkij', grouped, key_rows.astype(jnp.float32)) * head_dim ** (-0.5)
    allowed = jnp.arange(key_rows.shape[0])[None, :] <= first_pos + jnp.arange(row_count)[:, None]
    scores = jnp.where(allowed, scores, -1e+30)
    row_peak = lax.optimization_barrier(jnp.max(scores, axis=-1, keepdims=True))
    row_total = lax.optimization_barrier(jnp.sum(jnp.exp(scores - row_peak), axis=-1, keepdims=True))
    log_total = row_peak + jnp.log(row_total)
    weights = jnp.where(allowed, jnp.exp(scores - log_total), 0.0).astype(jnp.bfloat16)
    attended = jnp.einsum('gkij,jgd->igkd', weights.astype(jnp.float32), value_rows.astype(jnp.float32))
    return (attended.astype(jnp.bfloat16).reshape(row_count, head_count, head_dim), log_total[..., 0])

def attend_block_back(queries, key_rows, value_rows, log_total, attended, grad_attended, first_pos, head_dim):
    row_count, head_count = (queries.shape[0], queries.shape[1])
    groups = key_rows.shape[1]
    score_scale = head_dim ** (-0.5)
    grouped = queries.astype(jnp.float32).reshape(row_count, groups, head_count // groups, head_dim)
    grad_grouped = grad_attended.astype(jnp.float32).reshape(row_count, groups, head_count // groups, head_dim)
    key_float = key_rows.astype(jnp.float32)
    value_float = value_rows.astype(jnp.float32)
    scores = jnp.einsum('igkd,jgd->gkij', grouped, key_float) * score_scale
    allowed = jnp.arange(key_rows.shape[0])[None, :] <= first_pos + jnp.arange(row_count)[:, None]
    prob_rows = jnp.where(allowed, jnp.exp(jnp.where(allowed, scores, -1e+30) - log_total[..., None]), 0.0)
    row_delta = lax.optimization_barrier(jnp.sum(grad_grouped * attended.astype(jnp.float32).reshape(grad_grouped.shape), axis=-1))
    row_delta = jnp.transpose(row_delta, (1, 2, 0))[..., None]
    weights = prob_rows.astype(jnp.bfloat16).astype(jnp.float32)
    grad_values = jnp.einsum('gkij,igkd->jgd', weights, grad_grouped)
    grad_probs = jnp.einsum('igkd,jgd->gkij', grad_grouped, value_float)
    grad_scores = (prob_rows * (grad_probs - row_delta)).astype(jnp.bfloat16).astype(jnp.float32)
    grad_queries = jnp.einsum('gkij,jgd->igkd', grad_scores, key_float).reshape(row_count, head_count, head_dim) * score_scale
    grad_keys = jnp.einsum('gkij,igkd->jgd', grad_scores, grouped) * score_scale
    return (grad_queries, grad_keys, grad_values)

def reference(x_in, cotangent, conv_gain, conv_input, conv_kernel, conv_output, feed_gain_a, gate_first, up_first, down_first, attend_gain, query_weight, key_weight, value_weight, query_gain, key_gain, output_weight, feed_gain_b, gate_second, up_second, down_second):
    sequences, length, model_width = x_in.shape
    token_count = sequences * length
    head_dim = HD
    stream_zero = x_in.reshape(token_count, model_width)
    normed_one, inv_one, scaled_one = norm_forward(stream_zero, conv_gain)
    scaled_one = scaled_one.astype(jnp.bfloat16)
    projected = matmul(scaled_one, conv_input.reshape(model_width, 3 * model_width)).reshape(sequences, length, 3, model_width)
    gate_b = projected[:, :, 0]
    gate_c = projected[:, :, 1]
    inputs_x = projected[:, :, 2]
    product = gate_b * inputs_x
    padded = jnp.concatenate([jnp.zeros((sequences, 2, model_width), jnp.float32), product], axis=1)
    convolved = conv_kernel[0] * padded[:, :length] + conv_kernel[1] * padded[:, 1:length + 1] + conv_kernel[2] * padded[:, 2:]
    gated = (gate_c * convolved).astype(jnp.bfloat16).reshape(token_count, model_width)
    stream_one = stream_zero + matmul(gated, conv_output)
    stream_two, feed_saved_a = feed_forward(stream_one, feed_gain_a, gate_first, up_first, down_first)
    normed_three, inv_three, scaled_three = norm_forward(stream_two, attend_gain)
    scaled_three = scaled_three.astype(jnp.bfloat16)
    cosine_table, sine_table = rope_tables(jnp.arange(length, dtype=jnp.int32), head_dim)
    query_raw = matmul(scaled_three, query_weight).reshape(sequences, length, H, head_dim)
    key_raw = matmul(scaled_three, key_weight).reshape(sequences, length, KVH, head_dim)
    value_low = matmul(scaled_three, value_weight).astype(jnp.bfloat16).reshape(sequences, length, KVH, head_dim)
    query_unit, query_inv, query_scaled = norm_forward(query_raw, query_gain)
    key_unit, key_inv, key_scaled = norm_forward(key_raw, key_gain)
    queries = rotate(query_scaled, cosine_table, sine_table).astype(jnp.bfloat16)
    key_low = rotate(key_scaled, cosine_table, sine_table).astype(jnp.bfloat16)
    row_count = min(512, length)
    count = length // row_count
    starts = jnp.arange(count, dtype=jnp.int32) * row_count
    attended_list = []
    log_list = []
    for seq_index in range(sequences):

        def one_block(pieces, seq_index=seq_index):
            return attend_block(pieces[0], key_low[seq_index], value_low[seq_index], pieces[1], head_dim)
        attended_seq, log_seq = lax.map(one_block, (queries[seq_index].reshape(count, row_count, H, head_dim), starts))
        attended_list.append(attended_seq)
        log_list.append(log_seq)
    attended = jnp.stack(attended_list).reshape(token_count, H * head_dim)
    stream_three = stream_two + matmul(attended, output_weight)
    stream_four, feed_saved_b = feed_forward(stream_three, feed_gain_b, gate_second, up_second, down_second)
    layer_out = stream_four.reshape(sequences, length, model_width)
    grad = cotangent.reshape(token_count, model_width)
    grad, gain_feed_b, feed_b_grads = feed_backward(grad, feed_saved_b, feed_gain_b, gate_second, up_second, down_second)
    grad_low = grad.astype(jnp.bfloat16)
    grad_output_weight = left_product(attended, grad_low)
    grad_attended = right_product(grad_low, output_weight).astype(jnp.bfloat16).reshape(sequences, length, H, head_dim)
    grad_query_list = []
    grad_key_list = []
    grad_value_list = []
    for seq_index in range(sequences):

        def back_step(carry, pieces, seq_index=seq_index):
            grad_queries, grad_keys, grad_values = attend_block_back(pieces[0], key_low[seq_index], value_low[seq_index], pieces[1], pieces[2], pieces[3], pieces[4], head_dim)
            return ((carry[0] + grad_keys, carry[1] + grad_values), grad_queries)
        zero_keys = jnp.zeros((length, KVH, head_dim), jnp.float32)
        (grad_key_seq, grad_value_seq), grad_query_seq = lax.scan(back_step, (zero_keys, zero_keys), (queries[seq_index].reshape(count, row_count, H, head_dim), log_list[seq_index], attended_list[seq_index], grad_attended[seq_index].reshape(count, row_count, H, head_dim), starts))
        grad_query_list.append(grad_query_seq.reshape(length, H, head_dim))
        grad_key_list.append(grad_key_seq)
        grad_value_list.append(grad_value_seq)
    grad_queries = jnp.stack(grad_query_list)
    grad_keys = jnp.stack(grad_key_list)
    grad_values = jnp.stack(grad_value_list)
    grad_query_raw, grad_query_gain = norm_backward(rotate_back(grad_queries, cosine_table, sine_table), query_unit, query_inv, query_gain)
    grad_key_raw, grad_key_gain = norm_backward(rotate_back(grad_keys, cosine_table, sine_table), key_unit, key_inv, key_gain)
    query_grad_low = grad_query_raw.astype(jnp.bfloat16).reshape(token_count, -1)
    key_grad_low = grad_key_raw.astype(jnp.bfloat16).reshape(token_count, -1)
    value_grad_low = grad_values.astype(jnp.bfloat16).reshape(token_count, -1)
    grad_query_weight = left_product(scaled_three, query_grad_low)
    grad_key_weight = left_product(scaled_three, key_grad_low)
    grad_value_weight = left_product(scaled_three, value_grad_low)
    grad_scaled = right_product(query_grad_low, query_weight) + right_product(key_grad_low, key_weight) + right_product(value_grad_low, value_weight)
    grad_stream, gain_attend = norm_backward(grad_scaled, normed_three, inv_three, attend_gain)
    grad = grad + grad_stream
    grad, gain_feed_a, feed_a_grads = feed_backward(grad, feed_saved_a, feed_gain_a, gate_first, up_first, down_first)
    grad_low = grad.astype(jnp.bfloat16)
    grad_conv_output = left_product(gated, grad_low)
    grad_gated = right_product(grad_low, conv_output).reshape(sequences, length, model_width)
    grad_c = grad_gated * convolved
    grad_conv = grad_gated * gate_c
    kernel_grad = jnp.stack([lax.optimization_barrier(jnp.sum(grad_conv * padded[:, offset:offset + length], axis=(0, 1))) for offset in range(3)])
    padded_back = jnp.concatenate([grad_conv, jnp.zeros((sequences, 2, model_width), jnp.float32)], axis=1)
    grad_product = conv_kernel[2] * grad_conv + conv_kernel[1] * padded_back[:, 1:length + 1] + conv_kernel[0] * padded_back[:, 2:]
    grad_project = jnp.stack([grad_product * inputs_x, grad_c, grad_product * gate_b], axis=2).astype(jnp.bfloat16).reshape(token_count, 3 * model_width)
    grad_conv_input = left_product(scaled_one, grad_project).reshape(model_width, 3, model_width)
    grad_scaled = right_product(grad_project, conv_input.reshape(model_width, 3 * model_width))
    grad_stream, gain_conv = norm_backward(grad_scaled, normed_one, inv_one, conv_gain)
    grad_input = (grad + grad_stream).reshape(sequences, length, model_width)
    return (layer_out, grad_input, gain_conv, grad_conv_input, kernel_grad, grad_conv_output, gain_feed_a, feed_a_grads[0], feed_a_grads[1], feed_a_grads[2], gain_attend, grad_query_weight, grad_key_weight, grad_value_weight, grad_query_gain, grad_key_gain, grad_output_weight, gain_feed_b, feed_b_grads[0], feed_b_grads[1], feed_b_grads[2])
```

```python
import jax
import jax.numpy as jnp
from jax import lax
from jax.sharding import PartitionSpec as P


EPSILON = 1e-05
THETA = 1000000.0


def from_behind(value, axis, steps):
    count = lax.axis_size(axis)
    leading, last = (max(0, -steps), min(count, count - steps))
    return lax.ppermute(value, axis, [(source, source + steps) for source in range(leading, last)])


def matmul(lhs_matrix, rhs_matrix):
    return jnp.dot(lhs_matrix, rhs_matrix, preferred_element_type=jnp.float32)


def left_product(lhs_matrix, rhs_matrix):
    return lax.dot_general(
        lhs_matrix, rhs_matrix, (((0,), (0,)), ((), ())), preferred_element_type=jnp.float32
    )


def right_product(lhs_matrix, rhs_matrix):
    return lax.dot_general(
        lhs_matrix, rhs_matrix, (((1,), (1,)), ((), ())), preferred_element_type=jnp.float32
    )


def partners(count, distance):
    return [(index, index ^ distance) for index in range(count)]


def swap(value, axis, distance):
    return lax.ppermute(value, axis, partners(lax.axis_size(axis), distance))


def bit_of(axis, distance):
    return (lax.axis_index(axis) // distance) % 2


def tensor_total(partial_sum):
    count = lax.axis_size("tp")
    if count == 1:
        return partial_sum
    rows, width = partial_sum.shape
    half = rows // 2
    bit = bit_of("tp", 1)
    low = partial_sum.astype(jnp.bfloat16)
    mine = lax.dynamic_slice(low, (bit * half, 0), (half, width))
    other = lax.dynamic_slice(low, ((1 - bit) * half, 0), (half, width))
    total = mine.astype(jnp.float32) + swap(other, "tp", 1).astype(jnp.float32)
    distance = 2
    while distance < count:
        rounded = lax.optimization_barrier(total.astype(jnp.bfloat16))
        total = rounded.astype(jnp.float32) + swap(rounded, "tp", distance).astype(jnp.float32)
        distance *= 2
    final = lax.optimization_barrier(total.astype(jnp.bfloat16))
    received = swap(final, "tp", 1)
    first = jnp.where(bit == 0, final, received)
    second = jnp.where(bit == 0, received, final)
    return jnp.concatenate([first, second], axis=0).astype(jnp.float32)


def doubled_total(value, axes):
    for axis in axes:
        distance = 1
        while distance < lax.axis_size(axis):
            value = value + swap(value, axis, distance)
            distance *= 2
    return value


def pick_blocks(matrix, low_bit, next_bit):
    count = lax.axis_size("seq")
    block = matrix.shape[1] // count
    parts = [
        lax.dynamic_slice(
            matrix, (0, (group * 4 + next_bit * 2 + low_bit) * block), (matrix.shape[0], block)
        )
        for group in range(count // 4)
    ]
    return jnp.concatenate(parts, axis=1)


def share_rows(matrix):
    low_bit = bit_of("seq", 1)
    next_bit = bit_of("seq", 2)
    keep = pick_blocks(matrix, low_bit, next_bit)
    give = pick_blocks(matrix, low_bit, 1 - next_bit)
    away = jnp.concatenate(
        [
            pick_blocks(matrix, 1 - low_bit, next_bit),
            pick_blocks(matrix, 1 - low_bit, 1 - next_bit),
        ],
        axis=1,
    )
    received = swap(away, "seq", 1)
    width = keep.shape[1]
    return (keep, give, received[:, :width], received[:, width:])


def share_columns(matrix):
    return (matrix, swap(matrix, "seq", 1))


def weight_gradient(row_parts, column_parts):
    keep, give, keep_far, give_far = row_parts
    near, far = column_parts
    count = lax.axis_size("seq")
    sent = (left_product(give, near) + left_product(give_far, far)).astype(jnp.bfloat16)
    total = left_product(keep, near) + left_product(keep_far, far)
    total = total + swap(sent, "seq", 2).astype(jnp.float32)
    width = total.shape[1]
    blocks = count // 4
    total = total.reshape(blocks, total.shape[0] // blocks, width)
    distance = 4
    while distance < count:
        bit = bit_of("seq", distance)
        halves = total.reshape(blocks // 2, 2, total.shape[1], width)
        mine = lax.dynamic_index_in_dim(halves, bit, 1, keepdims=False)
        other = lax.dynamic_index_in_dim(halves, 1 - bit, 1, keepdims=False)
        total = mine + swap(other.astype(jnp.bfloat16), "seq", distance).astype(jnp.float32)
        blocks //= 2
        distance *= 2
    return total[0]


def norm_forward(stream, norm_gain):
    inv_rms = lax.rsqrt(jnp.mean(stream * stream, axis=-1, keepdims=True) + EPSILON)
    normed = stream * inv_rms
    return (normed, inv_rms, normed * norm_gain)


def norm_backward(grad_scaled, normed, inv_rms, norm_gain):
    grad_normed = grad_scaled * norm_gain
    grad_gain = jnp.sum((grad_scaled * normed).reshape(-1, norm_gain.shape[0]), axis=0)
    grad_stream = inv_rms * (
        grad_normed - normed * jnp.mean(grad_normed * normed, axis=-1, keepdims=True)
    )
    return (grad_stream, grad_gain)


def feed_forward(stream, norm_gain, gate_weight, up_weight, down_weight):
    normed, inv_rms, scaled = norm_forward(stream, norm_gain)
    scaled = scaled.astype(jnp.bfloat16)
    gate_pre = matmul(scaled, gate_weight)
    up_pre = matmul(scaled, up_weight)
    hidden = (gate_pre * jax.nn.sigmoid(gate_pre) * up_pre).astype(jnp.bfloat16)
    result = stream + tensor_total(matmul(hidden, down_weight))
    shared = (share_rows(scaled), share_columns(hidden))
    return (result, (normed, inv_rms, shared, gate_pre, up_pre))


def feed_backward(grad_out, saved_state, norm_gain, gate_weight, up_weight, down_weight):
    normed, inv_rms, shared, gate_pre, up_pre = saved_state
    grad_low = grad_out.astype(jnp.bfloat16)
    grad_hidden = right_product(grad_low, down_weight)
    sigmoid_gate = jax.nn.sigmoid(gate_pre)
    grad_gate = (
        grad_hidden * up_pre * sigmoid_gate * (1.0 + gate_pre * (1.0 - sigmoid_gate))
    ).astype(jnp.bfloat16)
    grad_up = (grad_hidden * gate_pre * sigmoid_gate).astype(jnp.bfloat16)
    grad_scaled = tensor_total(
        right_product(grad_gate, gate_weight) + right_product(grad_up, up_weight)
    )
    grad_stream, grad_gain = norm_backward(grad_scaled, normed, inv_rms, norm_gain)
    scaled_parts, hidden_parts = shared
    weight_grads = (
        weight_gradient(scaled_parts, share_columns(grad_gate)),
        weight_gradient(scaled_parts, share_columns(grad_up)),
        weight_gradient(share_rows(grad_low), hidden_parts).T,
    )
    return (grad_out + grad_stream, grad_gain, weight_grads)


def mixer_forward(stream, norm_gain, conv_input, conv_kernel, conv_output, sequences, block_len):
    channels = conv_kernel.shape[1]
    normed, inv_rms, scaled = norm_forward(stream, norm_gain)
    scaled = scaled.astype(jnp.bfloat16)
    projected = matmul(scaled, conv_input.reshape(conv_input.shape[0], 3 * channels)).reshape(
        sequences, block_len, 3, channels
    )
    gate_b = projected[:, :, 0]
    gate_c = projected[:, :, 1]
    inputs_x = projected[:, :, 2]
    product = gate_b * inputs_x
    edge_rows = from_behind(product[:, block_len - 2 :], "seq", 1)
    padded = jnp.concatenate([edge_rows, product], axis=1)
    convolved = (
        conv_kernel[0] * padded[:, :block_len]
        + conv_kernel[1] * padded[:, 1 : block_len + 1]
        + conv_kernel[2] * padded[:, 2:]
    )
    gated = (gate_c * convolved).astype(jnp.bfloat16).reshape(sequences * block_len, channels)
    result = stream + tensor_total(matmul(gated, conv_output))
    shared = (share_rows(scaled), share_columns(gated))
    return (result, (normed, inv_rms, shared, gate_b, gate_c, inputs_x, padded, convolved))


def mixer_backward(
    grad_out, saved_state, norm_gain, conv_input, conv_kernel, conv_output, sequences, block_len
):
    normed, inv_rms, shared, gate_b, gate_c, inputs_x, padded, convolved = saved_state
    channels = conv_kernel.shape[1]
    grad_low = grad_out.astype(jnp.bfloat16)
    grad_gated = right_product(grad_low, conv_output).reshape(sequences, block_len, channels)
    grad_c = grad_gated * convolved
    grad_conv = grad_gated * gate_c
    kernel_grad = jnp.stack(
        [
            jnp.sum(grad_conv * padded[:, offset : offset + block_len], axis=(0, 1))
            for offset in range(3)
        ]
    )
    edge_back = from_behind(grad_conv[:, :2], "seq", -1)
    padded_back = jnp.concatenate([grad_conv, edge_back], axis=1)
    grad_product = (
        conv_kernel[2] * grad_conv
        + conv_kernel[1] * padded_back[:, 1 : block_len + 1]
        + conv_kernel[0] * padded_back[:, 2:]
    )
    grad_project = (
        jnp.stack([grad_product * inputs_x, grad_c, grad_product * gate_b], axis=2)
        .astype(jnp.bfloat16)
        .reshape(sequences * block_len, 3 * channels)
    )
    flat_input = conv_input.reshape(conv_input.shape[0], 3 * channels)
    grad_scaled = tensor_total(right_product(grad_project, flat_input))
    grad_stream, grad_gain = norm_backward(grad_scaled, normed, inv_rms, norm_gain)
    scaled_parts, gated_parts = shared
    grad_conv_input = weight_gradient(scaled_parts, share_columns(grad_project))
    grad_conv_output = weight_gradient(share_rows(grad_low), gated_parts).T
    return (grad_out + grad_stream, grad_gain, kernel_grad, grad_conv_input, grad_conv_output)


def rope_tables(positions, head_dim):
    half_dim = head_dim // 2
    frequency = THETA ** (-(2.0 * jnp.arange(half_dim, dtype=jnp.float32)) / head_dim)
    angles = positions.astype(jnp.float32)[:, None] * frequency[None, :]
    cosine_table = jnp.concatenate([jnp.cos(angles), jnp.cos(angles)], axis=-1)
    sine_table = jnp.concatenate([jnp.sin(angles), jnp.sin(angles)], axis=-1)
    return (cosine_table, sine_table)


def rotate(field, cosine_table, sine_table):
    half_dim = field.shape[-1] // 2
    turned = jnp.concatenate([-field[..., half_dim:], field[..., :half_dim]], axis=-1)
    return field * cosine_table[:, None, :] + turned * sine_table[:, None, :]


def rotate_back(grad_field, cosine_table, sine_table):
    half_dim = grad_field.shape[-1] // 2
    moved = grad_field * sine_table[:, None, :]
    turned = jnp.concatenate([moved[..., half_dim:], -moved[..., :half_dim]], axis=-1)
    return grad_field * cosine_table[:, None, :] + turned


def attend(queries, key_rows, value_rows, allowed, head_dim):
    row_count, head_count = (queries.shape[0], queries.shape[1])
    groups = key_rows.shape[1]
    grouped = queries.reshape(row_count, groups, head_count // groups, head_dim)
    scores = jnp.einsum(
        "igkd,jgd->gkij", grouped, key_rows, preferred_element_type=jnp.float32
    ) * head_dim ** (-0.5)
    scores = jnp.where(allowed, scores, -1e30)
    row_peak = jnp.max(scores, axis=-1, keepdims=True)
    row_total = jnp.sum(jnp.exp(scores - row_peak), axis=-1, keepdims=True)
    log_total = row_peak + jnp.log(row_total)
    weights = jnp.where(allowed, jnp.exp(scores - log_total), 0.0).astype(jnp.bfloat16)
    attended = jnp.einsum("gkij,jgd->igkd", weights, value_rows, preferred_element_type=jnp.float32)
    return (
        attended.astype(jnp.bfloat16).reshape(row_count, head_count, head_dim),
        log_total[..., 0],
    )


def attend_back(
    queries, key_rows, value_rows, log_total, attended, grad_attended, allowed, head_dim
):
    row_count, head_count = (queries.shape[0], queries.shape[1])
    groups = key_rows.shape[1]
    score_scale = head_dim ** (-0.5)
    grouped = queries.reshape(row_count, groups, head_count // groups, head_dim)
    grad_grouped = grad_attended.reshape(row_count, groups, head_count // groups, head_dim)
    scores = (
        jnp.einsum("igkd,jgd->gkij", grouped, key_rows, preferred_element_type=jnp.float32)
        * score_scale
    )
    prob_rows = jnp.where(
        allowed, jnp.exp(jnp.where(allowed, scores, -1e30) - log_total[..., None]), 0.0
    )
    row_delta = jnp.sum(
        grad_grouped.astype(jnp.float32) * attended.reshape(grad_grouped.shape).astype(jnp.float32),
        axis=-1,
    )
    row_delta = jnp.transpose(row_delta, (1, 2, 0))[..., None]
    grad_values = jnp.einsum(
        "gkij,igkd->jgd",
        prob_rows.astype(jnp.bfloat16),
        grad_grouped,
        preferred_element_type=jnp.float32,
    )
    grad_probs = jnp.einsum(
        "igkd,jgd->gkij", grad_grouped, value_rows, preferred_element_type=jnp.float32
    )
    grad_scores = (prob_rows * (grad_probs - row_delta)).astype(jnp.bfloat16)
    grad_queries = (
        jnp.einsum(
            "gkij,jgd->igkd", grad_scores, key_rows, preferred_element_type=jnp.float32
        ).reshape(row_count, head_count, head_dim)
        * score_scale
    )
    grad_keys = (
        jnp.einsum("gkij,igkd->jgd", grad_scores, grouped, preferred_element_type=jnp.float32)
        * score_scale
    )
    return (grad_queries, grad_keys, grad_values)


def body(
    x_in,
    cotangent,
    conv_gain,
    conv_input,
    conv_kernel,
    conv_output,
    feed_gain_a,
    gate_first,
    up_first,
    down_first,
    attend_gain,
    query_weight,
    key_weight,
    value_weight,
    query_gain,
    key_gain,
    output_weight,
    feed_gain_b,
    gate_second,
    up_second,
    down_second,
):
    sequences, block_len, width = x_in.shape
    tokens = sequences * block_len
    head_dim = query_gain.shape[0]
    groups = key_weight.shape[1] // head_dim
    channels = conv_kernel.shape[1]
    stream_zero = x_in.reshape(tokens, width)
    stream_one, mixer_saved = mixer_forward(
        stream_zero, conv_gain, conv_input, conv_kernel, conv_output, sequences, block_len
    )
    stream_two, saved_a = feed_forward(stream_one, feed_gain_a, gate_first, up_first, down_first)
    normed_three, inv_three, scaled_three = norm_forward(stream_two, attend_gain)
    scaled_three = scaled_three.astype(jnp.bfloat16)
    first_pos = lax.axis_index("seq") * block_len
    cosine_table, sine_table = rope_tables(
        first_pos + jnp.arange(block_len, dtype=jnp.int32), head_dim
    )
    query_raw = matmul(scaled_three, query_weight).reshape(sequences, block_len, -1, head_dim)
    key_raw = matmul(scaled_three, key_weight).reshape(sequences, block_len, groups, head_dim)
    value_low = (
        matmul(scaled_three, value_weight)
        .astype(jnp.bfloat16)
        .reshape(sequences, block_len, groups, head_dim)
    )
    query_unit, query_inv, query_scaled = norm_forward(query_raw, query_gain)
    key_unit, key_inv, key_scaled = norm_forward(key_raw, key_gain)
    queries = rotate(query_scaled, cosine_table, sine_table).astype(jnp.bfloat16)
    key_low = rotate(key_scaled, cosine_table, sine_table).astype(jnp.bfloat16)
    count = lax.axis_size("seq")
    packed = jnp.stack([key_low, value_low])
    gathered = jnp.concatenate(
        [packed] + [swap(packed, "seq", distance) for distance in range(1, count)], axis=2
    )
    key_all, value_all = (gathered[0], gathered[1])
    sources = lax.axis_index("seq") ^ jnp.arange(count, dtype=jnp.int32)
    key_positions = (
        sources[:, None] * block_len + jnp.arange(block_len, dtype=jnp.int32)[None, :]
    ).reshape(-1)
    allowed = (
        key_positions[None, :] <= first_pos + jnp.arange(block_len, dtype=jnp.int32)[:, None]
    )
    attended_list = []
    log_list = []
    for seq_index in range(sequences):
        attended_seq, log_seq = attend(
            queries[seq_index], key_all[seq_index], value_all[seq_index], allowed, head_dim
        )
        attended_list.append(attended_seq)
        log_list.append(log_seq)
    attended = jnp.stack(attended_list).reshape(tokens, -1)
    attended_parts = share_columns(attended)
    scaled_parts = share_rows(scaled_three)
    stream_three = stream_two + tensor_total(matmul(attended, output_weight))
    stream_four, saved_b = feed_forward(
        stream_three, feed_gain_b, gate_second, up_second, down_second
    )
    layer_out = stream_four.reshape(sequences, block_len, width)
    grad = cotangent.reshape(tokens, width)
    grad, gain_feed_b, grads_b = feed_backward(
        grad, saved_b, feed_gain_b, gate_second, up_second, down_second
    )
    grad_low = grad.astype(jnp.bfloat16)
    grad_output_weight = weight_gradient(share_rows(grad_low), attended_parts).T
    grad_attended = (
        right_product(grad_low, output_weight)
        .astype(jnp.bfloat16)
        .reshape(sequences, block_len, -1, head_dim)
    )
    key_back, value_back = (key_all, value_all)
    query_grad_list = []
    key_grad_list = []
    value_grad_list = []
    for seq_index in range(sequences):
        grad_q, grad_k, grad_v = attend_back(
            queries[seq_index],
            key_back[seq_index],
            value_back[seq_index],
            log_list[seq_index],
            attended_list[seq_index],
            grad_attended[seq_index],
            allowed,
            head_dim,
        )
        query_grad_list.append(grad_q)
        key_grad_list.append(grad_k)
        value_grad_list.append(grad_v)
    grad_queries = jnp.stack(query_grad_list)
    key_value = jnp.stack([jnp.stack(key_grad_list), jnp.stack(value_grad_list)]).astype(
        jnp.bfloat16
    )
    key_value = key_value.reshape(2, sequences, count, block_len, groups, head_dim)
    arrived = [
        swap(key_value[:, :, distance], "seq", distance) for distance in range(1, count)
    ]
    key_value_sum = key_value[:, :, 0].astype(jnp.float32)
    for piece in arrived:
        key_value_sum = key_value_sum + piece.astype(jnp.float32)
    grad_keys, grad_values = (key_value_sum[0], key_value_sum[1])
    grad_query_raw, grad_query_gain = norm_backward(
        rotate_back(grad_queries, cosine_table, sine_table), query_unit, query_inv, query_gain
    )
    grad_key_raw, grad_key_gain = norm_backward(
        rotate_back(grad_keys, cosine_table, sine_table), key_unit, key_inv, key_gain
    )
    query_grad_low = grad_query_raw.astype(jnp.bfloat16).reshape(tokens, -1)
    key_grad_low = grad_key_raw.astype(jnp.bfloat16).reshape(tokens, -1)
    value_grad_low = grad_values.astype(jnp.bfloat16).reshape(tokens, -1)
    grad_scaled = tensor_total(
        right_product(query_grad_low, query_weight)
        + right_product(key_grad_low, key_weight)
        + right_product(value_grad_low, value_weight)
    )
    grad_stream, gain_attend = norm_backward(grad_scaled, normed_three, inv_three, attend_gain)
    grad = grad + grad_stream
    grad, gain_feed_a, grads_a = feed_backward(
        grad, saved_a, feed_gain_a, gate_first, up_first, down_first
    )
    grad, gain_conv, kernel_grad, grad_conv_input, grad_conv_output = mixer_backward(
        grad, mixer_saved, conv_gain, conv_input, conv_kernel, conv_output, sequences, block_len
    )
    grad_input = grad.reshape(sequences, block_len, width)
    projected_grad = weight_gradient(
        scaled_parts,
        share_columns(jnp.concatenate([query_grad_low, key_grad_low, value_grad_low], axis=1)),
    )
    query_width = query_grad_low.shape[1]
    key_width = key_grad_low.shape[1]
    kernel_full = lax.dynamic_update_slice(
        jnp.zeros((3, width), jnp.float32),
        kernel_grad,
        (jnp.zeros((), jnp.int32), lax.axis_index("tp") * channels),
    )
    over_seq = jnp.concatenate([gain_conv, gain_feed_a, gain_attend, gain_feed_b])
    over_both = jnp.concatenate([kernel_full.reshape(-1), grad_query_gain, grad_key_gain])
    over_both = doubled_total(over_both, ("tp",))
    merged = doubled_total(jnp.concatenate([over_seq, over_both]), ("seq",))
    kernel_at = 4 * width
    gain_at = kernel_at + 3 * width
    return (
        layer_out,
        grad_input,
        merged[:width],
        grad_conv_input.reshape(-1, 3, channels),
        merged[kernel_at:gain_at].reshape(3, width),
        grad_conv_output,
        merged[width : 2 * width],
        grads_a[0],
        grads_a[1],
        grads_a[2],
        merged[2 * width : 3 * width],
        projected_grad[:, :query_width],
        projected_grad[:, query_width : query_width + key_width],
        projected_grad[:, query_width + key_width :],
        merged[gain_at : gain_at + head_dim],
        merged[gain_at + head_dim :],
        grad_output_weight,
        merged[3 * width : 4 * width],
        grads_b[0],
        grads_b[1],
        grads_b[2],
    )


def solution(mesh):
    return jax.shard_map(
        body,
        mesh=mesh,
        in_specs=(
            P(None, "seq", None),
            P(None, "seq", None),
            P(),
            P(None, None, "tp"),
            P(None, "tp"),
            P("tp", None),
            P(),
            P(None, "tp"),
            P(None, "tp"),
            P("tp", None),
            P(),
            P(None, "tp"),
            P(None, "tp"),
            P(None, "tp"),
            P(),
            P(),
            P("tp", None),
            P(),
            P(None, "tp"),
            P(None, "tp"),
            P("tp", None),
        ),
        out_specs=(
            P(None, "seq", None),
            P(None, "seq", None),
            P(),
            P("seq", None, "tp"),
            P(),
            P("tp", "seq"),
            P(),
            P("seq", "tp"),
            P("seq", "tp"),
            P("tp", "seq"),
            P(),
            P("seq", "tp"),
            P("seq", "tp"),
            P("seq", "tp"),
            P(),
            P(),
            P("tp", "seq"),
            P(),
            P("seq", "tp"),
            P("seq", "tp"),
            P("tp", "seq"),
        ),
        check_vma=False,
    )
```

```python
import jax
import jax.numpy as jnp
from jax import lax
from jax.sharding import PartitionSpec as P


EPSILON = 1e-05
THETA = 1000000.0


def from_behind(value, axis, steps):
    count = lax.axis_size(axis)
    leading, last = (max(0, -steps), min(count, count - steps))
    return lax.ppermute(value, axis, [(source, source + steps) for source in range(leading, last)])


def matmul(lhs_matrix, rhs_matrix):
    return jnp.dot(lhs_matrix, rhs_matrix, preferred_element_type=jnp.float32)


def left_product(lhs_matrix, rhs_matrix):
    return lax.dot_general(
        lhs_matrix, rhs_matrix, (((0,), (0,)), ((), ())), preferred_element_type=jnp.float32
    )


def right_product(lhs_matrix, rhs_matrix):
    return lax.dot_general(
        lhs_matrix, rhs_matrix, (((1,), (1,)), ((), ())), preferred_element_type=jnp.float32
    )


def partners(count, distance):
    return [(index, index ^ distance) for index in range(count)]


def swap(value, axis, distance):
    return lax.ppermute(value, axis, partners(lax.axis_size(axis), distance))


def bit_of(axis, distance):
    return (lax.axis_index(axis) // distance) % 2


def after(value, token):
    return lax.optimization_barrier((value, token))[0]


def tensor_total(partial_sum):
    count = lax.axis_size("tp")
    if count == 1:
        return (partial_sum, partial_sum)
    rows, width = partial_sum.shape
    half = rows // 2
    bit = bit_of("tp", 1)
    low = partial_sum.astype(jnp.bfloat16)
    mine = lax.dynamic_slice(low, (bit * half, 0), (half, width))
    other = lax.dynamic_slice(low, ((1 - bit) * half, 0), (half, width))
    total = mine.astype(jnp.float32) + swap(other, "tp", 1).astype(jnp.float32)
    distance = 2
    token = other
    while distance < count:
        rounded = lax.optimization_barrier(total.astype(jnp.bfloat16))
        token = rounded
        total = rounded.astype(jnp.float32) + swap(rounded, "tp", distance).astype(jnp.float32)
        distance *= 2
    final = lax.optimization_barrier(total.astype(jnp.bfloat16))
    received = swap(final, "tp", 1)
    first = jnp.where(bit == 0, final, received)
    second = jnp.where(bit == 0, received, final)
    return (jnp.concatenate([first, second], axis=0).astype(jnp.float32), token)


def doubled_total(value, axes):
    for axis in axes:
        distance = 1
        while distance < lax.axis_size(axis):
            value = value + swap(value, axis, distance)
            distance *= 2
    return value


def order_blocks(matrix):
    count = lax.axis_size("seq")
    block = matrix.shape[1] // count
    low_bit = bit_of("seq", 1)
    next_bit = bit_of("seq", 2)
    pieces = [matrix[:, index * block : (index + 1) * block] for index in range(count)]
    ordered = []
    for low in range(2):
        for upper in range(2):
            for group in range(count // 4):
                base = 4 * group
                even = jnp.where(
                    next_bit == 0, pieces[base + 2 * upper], pieces[base + 2 - 2 * upper]
                )
                odd = jnp.where(
                    next_bit == 0, pieces[base + 2 * upper + 1], pieces[base + 3 - 2 * upper]
                )
                ordered.append(
                    jnp.where(low_bit == low, even, odd)
                )
    half = len(ordered) // 2
    return (jnp.concatenate(ordered[:half], axis=1), jnp.concatenate(ordered[half:], axis=1))


def share_rows(matrix):
    near, away = order_blocks(matrix)
    return (near, swap(away, "seq", 1))


def share_columns(matrix):
    return (matrix, swap(matrix, "seq", 1))


def left_parts(parts, which):
    near, far = parts
    half = near.shape[1] // 2
    return (
        near[:, which * half : (which + 1) * half],
        far[:, which * half : (which + 1) * half],
    )


def pair_product(row_parts, column_parts):
    return left_product(row_parts[0], column_parts[0]) + left_product(
        row_parts[1], column_parts[1]
    )


def begin_gradient(row_list, column_list):
    sent = [
        pair_product(left_parts(rows, 1), columns).astype(jnp.bfloat16)
        for rows, columns in zip(row_list, column_list)
    ]
    kept = [
        pair_product(left_parts(rows, 0), columns)
        for rows, columns in zip(row_list, column_list)
    ]
    sent = jnp.concatenate(sent, axis=1) if len(sent) > 1 else sent[0]
    kept = jnp.concatenate(kept, axis=1) if len(kept) > 1 else kept[0]
    return (kept, swap(sent, "seq", 2))


def middle_gradient(kept, arrived):
    count = lax.axis_size("seq")
    total = kept + arrived.astype(jnp.float32)
    width = total.shape[1]
    blocks = count // 4
    block = total.shape[0] // blocks
    distance = 4
    arrived = None
    while distance < count:
        if arrived is not None:
            total = total + arrived.astype(jnp.float32)
        bit = bit_of("seq", distance)
        halves = total.reshape(blocks // 2, 2, block, width)
        total = lax.dynamic_index_in_dim(halves, bit, 1, keepdims=False)
        other = lax.dynamic_index_in_dim(halves, 1 - bit, 1, keepdims=False)
        arrived = swap(other.astype(jnp.bfloat16), "seq", distance)
        blocks //= 2
        distance *= 2
    if arrived is None:
        arrived = jnp.zeros_like(total)
    return (total.reshape(block, width), arrived.reshape(block, width))


def finish_gradient(total, arrived):
    return total + arrived.astype(jnp.float32)


def norm_forward(stream, norm_gain):
    inv_rms = lax.rsqrt(jnp.mean(stream * stream, axis=-1, keepdims=True) + EPSILON)
    normed = stream * inv_rms
    return (normed, inv_rms, normed * norm_gain)


def norm_backward(grad_scaled, normed, inv_rms, norm_gain):
    grad_normed = grad_scaled * norm_gain
    grad_gain = jnp.sum((grad_scaled * normed).reshape(-1, norm_gain.shape[0]), axis=0)
    grad_stream = inv_rms * (
        grad_normed - normed * jnp.mean(grad_normed * normed, axis=-1, keepdims=True)
    )
    return (grad_stream, grad_gain)


def feed_forward(stream, norm_gain, gate_weight, up_weight, down_weight):
    normed, inv_rms, scaled = norm_forward(stream, norm_gain)
    scaled = scaled.astype(jnp.bfloat16)
    gate_pre = matmul(scaled, gate_weight)
    up_pre = matmul(scaled, up_weight)
    hidden = (gate_pre * jax.nn.sigmoid(gate_pre) * up_pre).astype(jnp.bfloat16)
    addition, token = tensor_total(matmul(hidden, down_weight))
    result = stream + addition
    shared = (share_rows(scaled), share_columns(hidden))
    return (result, (normed, inv_rms, shared, gate_pre, up_pre), token)


def feed_backward(grad_out, saved_state, norm_gain, gate_weight, up_weight, down_weight):
    normed, inv_rms, shared, gate_pre, up_pre = saved_state
    grad_low = grad_out.astype(jnp.bfloat16)
    grad_hidden = right_product(grad_low, down_weight)
    sigmoid_gate = jax.nn.sigmoid(gate_pre)
    grad_gate = (
        grad_hidden * up_pre * sigmoid_gate * (1.0 + gate_pre * (1.0 - sigmoid_gate))
    ).astype(jnp.bfloat16)
    grad_up = (grad_hidden * gate_pre * sigmoid_gate).astype(jnp.bfloat16)
    column_parts = (
        share_columns(jnp.concatenate([grad_gate, grad_up], axis=1)),
        share_rows(grad_low),
    )
    grad_scaled, token = tensor_total(
        right_product(grad_gate, gate_weight) + right_product(grad_up, up_weight)
    )
    grad_stream, grad_gain = norm_backward(grad_scaled, normed, inv_rms, norm_gain)
    return (grad_out + grad_stream, grad_gain, shared, column_parts, token)


def feed_begin(shared, column_parts, token):
    scaled_parts, hidden_parts = shared
    both, low = column_parts
    both = (both[0], after(both[1], token))
    low = (low[0], after(low[1], token))
    return (
        begin_gradient([scaled_parts], [both]),
        begin_gradient([low], [hidden_parts]),
    )


def feed_middle(stages, token):
    return tuple(middle_gradient(kept, after(arrived, token)) for kept, arrived in stages)


def feed_finish(stages, token):
    both, down = [finish_gradient(total, after(arrived, token)) for total, arrived in stages]
    width = both.shape[1] // 2
    return (both[:, :width], both[:, width:], down.T)


def mixer_forward(stream, norm_gain, conv_input, conv_kernel, conv_output, sequences, block_len):
    channels = conv_kernel.shape[1]
    normed, inv_rms, scaled = norm_forward(stream, norm_gain)
    scaled = scaled.astype(jnp.bfloat16)
    projected = matmul(scaled, conv_input.reshape(conv_input.shape[0], 3 * channels)).reshape(
        sequences, block_len, 3, channels
    )
    gate_b = projected[:, :, 0]
    gate_c = projected[:, :, 1]
    inputs_x = projected[:, :, 2]
    product = gate_b * inputs_x
    edge_rows = from_behind(product[:, block_len - 2 :], "seq", 1)
    padded = jnp.concatenate([edge_rows, product], axis=1)
    convolved = (
        conv_kernel[0] * padded[:, :block_len]
        + conv_kernel[1] * padded[:, 1 : block_len + 1]
        + conv_kernel[2] * padded[:, 2:]
    )
    gated = (gate_c * convolved).astype(jnp.bfloat16).reshape(sequences * block_len, channels)
    addition, token = tensor_total(matmul(gated, conv_output))
    result = stream + addition
    shared = (share_rows(scaled), share_columns(gated))
    return (result, (normed, inv_rms, shared, gate_b, gate_c, inputs_x, padded, convolved))


def mixer_backward(
    grad_out, saved_state, norm_gain, conv_input, conv_kernel, conv_output, sequences, block_len
):
    normed, inv_rms, shared, gate_b, gate_c, inputs_x, padded, convolved = saved_state
    channels = conv_kernel.shape[1]
    grad_low = grad_out.astype(jnp.bfloat16)
    grad_gated = right_product(grad_low, conv_output).reshape(sequences, block_len, channels)
    grad_c = grad_gated * convolved
    grad_conv = grad_gated * gate_c
    kernel_grad = jnp.stack(
        [
            jnp.sum(grad_conv * padded[:, offset : offset + block_len], axis=(0, 1))
            for offset in range(3)
        ]
    )
    edge_back = from_behind(grad_conv[:, :2], "seq", -1)
    padded_back = jnp.concatenate([grad_conv, edge_back], axis=1)
    grad_product = (
        conv_kernel[2] * grad_conv
        + conv_kernel[1] * padded_back[:, 1 : block_len + 1]
        + conv_kernel[0] * padded_back[:, 2:]
    )
    grad_project = (
        jnp.stack([grad_product * inputs_x, grad_c, grad_product * gate_b], axis=2)
        .astype(jnp.bfloat16)
        .reshape(sequences * block_len, 3 * channels)
    )
    flat_input = conv_input.reshape(conv_input.shape[0], 3 * channels)
    column_parts = (share_columns(grad_project), share_rows(grad_low))
    grad_scaled, token = tensor_total(right_product(grad_project, flat_input))
    grad_stream, grad_gain = norm_backward(grad_scaled, normed, inv_rms, norm_gain)
    return (grad_out + grad_stream, grad_gain, kernel_grad, shared, column_parts, token)


def rope_tables(positions, head_dim):
    half_dim = head_dim // 2
    frequency = THETA ** (-(2.0 * jnp.arange(half_dim, dtype=jnp.float32)) / head_dim)
    angles = positions.astype(jnp.float32)[:, None] * frequency[None, :]
    cosine_table = jnp.concatenate([jnp.cos(angles), jnp.cos(angles)], axis=-1)
    sine_table = jnp.concatenate([jnp.sin(angles), jnp.sin(angles)], axis=-1)
    return (cosine_table, sine_table)


def rotate(field, cosine_table, sine_table):
    half_dim = field.shape[-1] // 2
    turned = jnp.concatenate([-field[..., half_dim:], field[..., :half_dim]], axis=-1)
    return field * cosine_table[:, None, :] + turned * sine_table[:, None, :]


def rotate_back(grad_field, cosine_table, sine_table):
    half_dim = grad_field.shape[-1] // 2
    moved = grad_field * sine_table[:, None, :]
    turned = jnp.concatenate([moved[..., half_dim:], -moved[..., :half_dim]], axis=-1)
    return grad_field * cosine_table[:, None, :] + turned


def attend(queries, key_rows, value_rows, allowed, head_dim):
    row_count, head_count = (queries.shape[0], queries.shape[1])
    groups = key_rows.shape[1]
    grouped = queries.reshape(row_count, groups, head_count // groups, head_dim)
    scores = jnp.einsum(
        "igkd,jgd->gkij", grouped, key_rows, preferred_element_type=jnp.float32
    ) * head_dim ** (-0.5)
    scores = jnp.where(allowed, scores, -1e30)
    row_peak = jnp.max(scores, axis=-1, keepdims=True)
    row_total = jnp.sum(jnp.exp(scores - row_peak), axis=-1, keepdims=True)
    log_total = row_peak + jnp.log(row_total)
    weights = jnp.where(allowed, jnp.exp(scores - log_total), 0.0).astype(jnp.bfloat16)
    attended = jnp.einsum("gkij,jgd->igkd", weights, value_rows, preferred_element_type=jnp.float32)
    return (
        attended.astype(jnp.bfloat16).reshape(row_count, head_count, head_dim),
        log_total[..., 0],
    )


def attend_back(
    queries, key_rows, value_rows, log_total, attended, grad_attended, allowed, head_dim
):
    row_count, head_count = (queries.shape[0], queries.shape[1])
    groups = key_rows.shape[1]
    score_scale = head_dim ** (-0.5)
    grouped = queries.reshape(row_count, groups, head_count // groups, head_dim)
    grad_grouped = grad_attended.reshape(row_count, groups, head_count // groups, head_dim)
    scores = (
        jnp.einsum("igkd,jgd->gkij", grouped, key_rows, preferred_element_type=jnp.float32)
        * score_scale
    )
    prob_rows = jnp.where(
        allowed, jnp.exp(jnp.where(allowed, scores, -1e30) - log_total[..., None]), 0.0
    )
    row_delta = jnp.sum(
        grad_grouped.astype(jnp.float32) * attended.reshape(grad_grouped.shape).astype(jnp.float32),
        axis=-1,
    )
    row_delta = jnp.transpose(row_delta, (1, 2, 0))[..., None]
    grad_values = jnp.einsum(
        "gkij,igkd->jgd",
        prob_rows.astype(jnp.bfloat16),
        grad_grouped,
        preferred_element_type=jnp.float32,
    )
    grad_probs = jnp.einsum(
        "igkd,jgd->gkij", grad_grouped, value_rows, preferred_element_type=jnp.float32
    )
    grad_scores = (prob_rows * (grad_probs - row_delta)).astype(jnp.bfloat16)
    grad_queries = (
        jnp.einsum(
            "gkij,jgd->igkd", grad_scores, key_rows, preferred_element_type=jnp.float32
        ).reshape(row_count, head_count, head_dim)
        * score_scale
    )
    grad_keys = (
        jnp.einsum("gkij,igkd->jgd", grad_scores, grouped, preferred_element_type=jnp.float32)
        * score_scale
    )
    return (grad_queries, grad_keys, grad_values)


def body(
    x_in,
    cotangent,
    conv_gain,
    conv_input,
    conv_kernel,
    conv_output,
    feed_gain_a,
    gate_first,
    up_first,
    down_first,
    attend_gain,
    query_weight,
    key_weight,
    value_weight,
    query_gain,
    key_gain,
    output_weight,
    feed_gain_b,
    gate_second,
    up_second,
    down_second,
):
    sequences, block_len, width = x_in.shape
    tokens = sequences * block_len
    head_dim = query_gain.shape[0]
    groups = key_weight.shape[1] // head_dim
    channels = conv_kernel.shape[1]
    stream_zero = x_in.reshape(tokens, width)
    stream_one, mixer_saved = mixer_forward(
        stream_zero, conv_gain, conv_input, conv_kernel, conv_output, sequences, block_len
    )
    stream_two, saved_a, _ = feed_forward(stream_one, feed_gain_a, gate_first, up_first, down_first)
    normed_three, inv_three, scaled_three = norm_forward(stream_two, attend_gain)
    scaled_three = scaled_three.astype(jnp.bfloat16)
    first_pos = lax.axis_index("seq") * block_len
    cosine_table, sine_table = rope_tables(
        first_pos + jnp.arange(block_len, dtype=jnp.int32), head_dim
    )
    query_raw = matmul(scaled_three, query_weight).reshape(sequences, block_len, -1, head_dim)
    key_raw = matmul(scaled_three, key_weight).reshape(sequences, block_len, groups, head_dim)
    value_low = (
        matmul(scaled_three, value_weight)
        .astype(jnp.bfloat16)
        .reshape(sequences, block_len, groups, head_dim)
    )
    query_unit, query_inv, query_scaled = norm_forward(query_raw, query_gain)
    key_unit, key_inv, key_scaled = norm_forward(key_raw, key_gain)
    queries = rotate(query_scaled, cosine_table, sine_table).astype(jnp.bfloat16)
    key_low = rotate(key_scaled, cosine_table, sine_table).astype(jnp.bfloat16)
    count = lax.axis_size("seq")
    packed = jnp.stack([key_low, value_low])
    gathered = packed
    distances = [0]
    distance = count // 2
    while distance:
        gathered = jnp.concatenate([gathered, swap(gathered, "seq", distance)], axis=2)
        distances = distances + [index ^ distance for index in distances]
        distance //= 2
    key_all, value_all = (gathered[0], gathered[1])
    sources = lax.axis_index("seq") ^ jnp.array(distances, dtype=jnp.int32)
    key_positions = (
        sources[:, None] * block_len + jnp.arange(block_len, dtype=jnp.int32)[None, :]
    ).reshape(-1)
    allowed = (
        key_positions[None, :] <= first_pos + jnp.arange(block_len, dtype=jnp.int32)[:, None]
    )
    attended_list = []
    log_list = []
    for seq_index in range(sequences):
        attended_seq, log_seq = attend(
            queries[seq_index], key_all[seq_index], value_all[seq_index], allowed, head_dim
        )
        attended_list.append(attended_seq)
        log_list.append(log_seq)
    attended = jnp.stack(attended_list).reshape(tokens, -1)
    attended_parts = share_columns(attended)
    scaled_parts = share_rows(scaled_three)
    addition, token_three = tensor_total(matmul(attended, output_weight))
    stream_three = stream_two + addition
    stream_four, saved_b, _ = feed_forward(
        stream_three, feed_gain_b, gate_second, up_second, down_second
    )
    layer_out = stream_four.reshape(sequences, block_len, width)
    grad = cotangent.reshape(tokens, width)
    grad, gain_feed_b, shared_b, columns_b, _ = feed_backward(
        grad, saved_b, feed_gain_b, gate_second, up_second, down_second
    )
    grad_low = grad.astype(jnp.bfloat16)
    output_rows = share_rows(grad_low)
    grad_attended = (
        right_product(grad_low, output_weight)
        .astype(jnp.bfloat16)
        .reshape(sequences, block_len, -1, head_dim)
    )
    key_back, value_back = (key_all, value_all)
    query_grad_list = []
    key_grad_list = []
    value_grad_list = []
    for seq_index in range(sequences):
        grad_q, grad_k, grad_v = attend_back(
            queries[seq_index],
            key_back[seq_index],
            value_back[seq_index],
            log_list[seq_index],
            attended_list[seq_index],
            grad_attended[seq_index],
            allowed,
            head_dim,
        )
        query_grad_list.append(grad_q)
        key_grad_list.append(grad_k)
        value_grad_list.append(grad_v)
    grad_queries = jnp.stack(query_grad_list)
    key_value = jnp.stack([jnp.stack(key_grad_list), jnp.stack(value_grad_list)]).astype(
        jnp.bfloat16
    )
    token = key_value
    key_value_sum = key_value.astype(jnp.float32)
    distance = 1
    while distance < count:
        half = key_value_sum.shape[2] // 2
        arrived = swap(key_value_sum[:, :, half:].astype(jnp.bfloat16), "seq", distance)
        key_value_sum = key_value_sum[:, :, :half] + arrived.astype(jnp.float32)
        distance *= 2
    stages_b = feed_begin(shared_b, columns_b, token)
    grad_keys, grad_values = (key_value_sum[0], key_value_sum[1])
    grad_query_raw, grad_query_gain = norm_backward(
        rotate_back(grad_queries, cosine_table, sine_table), query_unit, query_inv, query_gain
    )
    grad_key_raw, grad_key_gain = norm_backward(
        rotate_back(grad_keys, cosine_table, sine_table), key_unit, key_inv, key_gain
    )
    query_grad_low = grad_query_raw.astype(jnp.bfloat16).reshape(tokens, -1)
    key_grad_low = grad_key_raw.astype(jnp.bfloat16).reshape(tokens, -1)
    value_grad_low = grad_values.astype(jnp.bfloat16).reshape(tokens, -1)
    projected_parts = share_columns(
        jnp.concatenate([query_grad_low, key_grad_low, value_grad_low], axis=1)
    )
    grad_scaled, token = tensor_total(
        right_product(query_grad_low, query_weight)
        + right_product(key_grad_low, key_weight)
        + right_product(value_grad_low, value_weight)
    )
    stages_b = feed_middle(stages_b, token)
    grad_stream, gain_attend = norm_backward(grad_scaled, normed_three, inv_three, attend_gain)
    grad = grad + grad_stream
    grad, gain_feed_a, shared_a, columns_a, token = feed_backward(
        grad, saved_a, feed_gain_a, gate_first, up_first, down_first
    )
    grads_b = feed_finish(stages_b, token)
    projected_parts = (projected_parts[0], after(projected_parts[1], token))
    output_rows = (output_rows[0], after(output_rows[1], token))
    stages_c = begin_gradient([scaled_parts, output_rows], [projected_parts, attended_parts])
    stages_a = feed_begin(shared_a, columns_a, token)
    grad, gain_conv, kernel_grad, shared_m, columns_m, token = mixer_backward(
        grad, mixer_saved, conv_gain, conv_input, conv_kernel, conv_output, sequences, block_len
    )
    stages_c = middle_gradient(stages_c[0], after(stages_c[1], token))
    stages_a = feed_middle(stages_a, token)
    columns_m = [(near, after(far, token)) for near, far in columns_m]
    stages_m = begin_gradient([shared_m[0], columns_m[1]], [columns_m[0], shared_m[1]])
    grad_input = grad.reshape(sequences, block_len, width)
    projected_grad = finish_gradient(stages_c[0], after(stages_c[1], grad))
    grads_a = feed_finish(stages_a, grad)
    stages_m = middle_gradient(stages_m[0], after(stages_m[1], grad))
    mixer_grad = finish_gradient(*stages_m)
    query_width = query_grad_low.shape[1]
    key_width = key_grad_low.shape[1]
    split = query_width + 2 * key_width
    grad_output_weight = projected_grad[:, split:].T
    grad_conv_input = mixer_grad[:, : 3 * channels]
    grad_conv_output = mixer_grad[:, 3 * channels :].T
    kernel_full = lax.dynamic_update_slice(
        jnp.zeros((3, width), jnp.float32),
        kernel_grad,
        (jnp.zeros((), jnp.int32), lax.axis_index("tp") * channels),
    )
    over_seq = jnp.concatenate([gain_conv, gain_feed_a, gain_attend, gain_feed_b])
    over_both = jnp.concatenate([kernel_full.reshape(-1), grad_query_gain, grad_key_gain])
    over_both = doubled_total(over_both, ("tp",))
    merged = doubled_total(jnp.concatenate([over_seq, over_both]), ("seq",))
    kernel_at = 4 * width
    gain_at = kernel_at + 3 * width
    return (
        layer_out,
        grad_input,
        merged[:width],
        grad_conv_input.reshape(-1, 3, channels),
        merged[kernel_at:gain_at].reshape(3, width),
        grad_conv_output,
        merged[width : 2 * width],
        grads_a[0],
        grads_a[1],
        grads_a[2],
        merged[2 * width : 3 * width],
        projected_grad[:, :query_width],
        projected_grad[:, query_width : query_width + key_width],
        projected_grad[:, query_width + key_width : split],
        merged[gain_at : gain_at + head_dim],
        merged[gain_at + head_dim :],
        grad_output_weight,
        merged[3 * width : 4 * width],
        grads_b[0],
        grads_b[1],
        grads_b[2],
    )


def solution(mesh):
    return jax.shard_map(
        body,
        mesh=mesh,
        in_specs=(
            P(None, "seq", None),
            P(None, "seq", None),
            P(),
            P(None, None, "tp"),
            P(None, "tp"),
            P("tp", None),
            P(),
            P(None, "tp"),
            P(None, "tp"),
            P("tp", None),
            P(),
            P(None, "tp"),
            P(None, "tp"),
            P(None, "tp"),
            P(),
            P(),
            P("tp", None),
            P(),
            P(None, "tp"),
            P(None, "tp"),
            P("tp", None),
        ),
        out_specs=(
            P(None, "seq", None),
            P(None, "seq", None),
            P(),
            P("seq", None, "tp"),
            P(),
            P("tp", "seq"),
            P(),
            P("seq", "tp"),
            P("seq", "tp"),
            P("tp", "seq"),
            P(),
            P("seq", "tp"),
            P("seq", "tp"),
            P("seq", "tp"),
            P(),
            P(),
            P("tp", "seq"),
            P(),
            P("seq", "tp"),
            P("seq", "tp"),
            P("tp", "seq"),
        ),
        check_vma=False,
    )
```
